32 devices in a mesh: wide: 16 (over z, x, core), narrow: 2 (over y).
Axes of the slice: x: 2, y: 2, z: 4, core: 2. Of those that a mesh axis runs over, the one named last changes fastest.
Arguments:
- hess_inverse: bfloat16 [26880, 26880], P('wide', 'narrow'), may hold values from -0.0390625 to 0.0390625
- observations: bfloat16 [16, 26880], P('wide', 'narrow'), may hold values from -6 to 6
- adjoint_maps: bfloat16 [210, 2, 6144, 128], P('narrow', None, 'wide'), may hold values from -0.375 to 0.375
Outputs:
- estimate: float32 [6144, 210, 16], P(('wide', 'narrow'))
The draws below stay inside these ranges and needn't reach their ends.
All inputs are finite; a program needn't handle non-finite values.
Results may differ from the reference program's by a relative error of at most 0.004.
Values may be sent and summed in bfloat16 or wider, within the bound.
A program may use at most 128 MiB of HBM per device.

```python
import math
import jax
import jax.numpy as jnp
from jax import lax

S = 128
NT = 210
NF = 210
P_SIZE = 6144
SCEN = 16
NDATA = 26880


def block_levels(own_key, shape, pieces, smallest, high):
    level = 1.0
    for axis_at, parts in pieces:
        steps = jax.random.uniform(jax.random.fold_in(jax.random.fold_in(own_key, 6), axis_at), (parts,), jnp.float32, smallest / len(pieces), high / len(pieces))
        level = level * jnp.repeat(jnp.exp(steps), shape[axis_at] // parts).reshape((-1,) + (1,) * (len(shape) - 1 - axis_at))
    return level


def noise(stream_key, dims, scale, reach, split=(), held_as=jnp.bfloat16):
    values = scale * jax.random.normal(stream_key, dims, jnp.float32)
    if split:
        values = values * block_levels(stream_key, dims, split, -0.22, 0.18)
    return jnp.clip(values, -reach, reach).astype(held_as)


def setup_inputs(seed: int = 0) -> dict:
    key_list = jax.random.split(jax.random.key(seed), 4)
    hess_inverse = noise(key_list[0], (NDATA, NDATA), NDATA ** -0.5, 0.0390625, ((0, 16), (1, 2)))
    observations = noise(key_list[1], (SCEN, NDATA), 1.0, 6.0, ((0, 16), (1, 2)))
    adjoint_maps = noise(key_list[2], (NF, 2, P_SIZE, S), (2 * S * NT // NF) ** -0.5, 0.375, ((0, 2), (2, 16)))
    return dict(hess_inverse=hess_inverse, observations=observations, adjoint_maps=adjoint_maps)


full_turn = 2.0 * math.pi


def analysis_table():
    times_axis = jnp.arange(NT).astype(jnp.float32)
    freqs = jnp.arange(NF).astype(jnp.float32)
    angles = full_turn * times_axis[:, None] * freqs[None, :] / (2.0 * NF)
    return jnp.stack([jnp.cos(angles), -jnp.sin(angles)], axis=-1)


def synthesis_table():
    times_axis = jnp.arange(NT).astype(jnp.float32)
    freqs = jnp.arange(NF).astype(jnp.float32)
    angles = full_turn * freqs[:, None] * times_axis[None, :] / (2.0 * NF)
    return jnp.stack([jnp.cos(angles), -jnp.sin(angles)], axis=1)


def reference(hess_inverse, observations, adjoint_maps):
    highest = lax.Precision.HIGHEST
    observed = observations.astype(jnp.float32)
    block_rows = NDATA // 16
    blocks = hess_inverse.reshape(16, block_rows, NDATA)

    def apply_block(rows_block):
        return jnp.dot(observed, rows_block.astype(jnp.float32).T, precision=highest)

    products = lax.map(apply_block, blocks)
    series = jnp.transpose(products, (1, 0, 2)).reshape(SCEN, NDATA)
    values = series.reshape(SCEN, S, NT)
    spectra = jnp.einsum("nst,tfc->fcsn", values, analysis_table(), precision=highest).astype(jnp.bfloat16)
    spec = spectra.astype(jnp.float32)
    basis = synthesis_table()
    block_count = 8 if P_SIZE % 8 == 0 else 1
    param_block = P_SIZE // block_count
    map_blocks = jnp.transpose(adjoint_maps.reshape(NF, 2, block_count, param_block, S), (2, 0, 1, 3, 4))

    def block_estimate(maps):
        mapped = maps.astype(jnp.float32)
        real_part = jnp.einsum("fps,fsn->fpn", mapped[:, 0], spec[:, 0], precision=highest) - jnp.einsum("fps,fsn->fpn", mapped[:, 1], spec[:, 1], precision=highest)
        imag_part = jnp.einsum("fps,fsn->fpn", mapped[:, 0], spec[:, 1], precision=highest) + jnp.einsum("fps,fsn->fpn", mapped[:, 1], spec[:, 0], precision=highest)
        real_part = lax.optimization_barrier(real_part.astype(jnp.bfloat16)).astype(jnp.float32)
        imag_part = lax.optimization_barrier(imag_part.astype(jnp.bfloat16)).astype(jnp.float32)
        result = jnp.einsum("fpn,ft->ptn", real_part, basis[:, 0], precision=highest) + jnp.einsum("fpn,ft->ptn", imag_part, basis[:, 1], precision=highest)
        return result * (1.0 / NF)

    estimates = lax.map(block_estimate, map_blocks)
    return estimates.reshape(P_SIZE, NT, SCEN)
```

```python
import functools
import math

import jax
import jax.numpy as jnp
import numpy as np
from jax import lax
from jax.experimental import pallas as pl
from jax.experimental.pallas import tpu as pltpu
from jax.sharding import PartitionSpec as P

MESH = pl.DeviceIdType.MESH
LANES = 128
CHUNK = 256
GROUP = 16
EXTRA = 13
LEND = 4
STAGES = ((0, 2), (2, 2), (4, 2), (6, 1), (7, 1))


def angles(freqs, times, turn):
    return 2.0 * math.pi * ((freqs * times) % turn) / turn


def analysis_table(nt, nf):
    a = angles(np.arange(nt)[:, None], np.arange(nf)[None, :], 2 * nf)
    return np.stack([np.cos(a), -np.sin(a)], axis=1).astype(np.float32)


def synthesis_table(nt, nf):
    a = angles(np.arange(nf)[:, None], np.arange(nt)[None, :], 2 * nf)
    return np.stack([np.cos(a), -np.sin(a)], axis=1).astype(np.float32)


def layout(nf_dev):
    moved = nf_dev - EXTRA
    rest = moved % GROUP
    return [(moved, EXTRA, GROUP), (moved - rest, rest, 4 * -(-rest // 4))] + [
        (f, GROUP, GROUP) for f in range(0, moved - rest, GROUP)]


def main_kernel(zs, scen, nt, obs_ref, analysis_ref, synthesis_ref, hess_hbm, a_hbm, base_hbm, last_ref,
                table_out, hess, a, own32, mine, rows16, wide_op, part, came, series, gathered, flat, turned, m32, sent, m, laid,
                load, load_a, send_o, recv_o, send_n, recv_n, send_s, recv_s, send_m, recv_m, send_e, recv_e,
                leaving):
    w, k = lax.axis_index("wide"), lax.axis_index("narrow")
    z, x, c = w // 4, (w // 2) % 2, w % 2
    other = 1 - k
    slots_h, _, cols = hess.shape
    pieces, share, _ = mine.shape
    nf, _, points, sensors = a.shape
    half = points // 2
    rows = sensors // scen * nt
    full, rest = rows // CHUNK, rows % CHUNK
    local = rows // nt
    slots = layout(nf)
    moved = slots[0][0]
    groups = len(slots) - 2

    def at(zz, xx, cc):
        return (zz * 2 + xx) * 2 + cc

    def chunk_rows(g):
        return rest if isinstance(g, int) and g == full else CHUNK

    def fetch(g, size):
        lines = pl.ds(pl.multiple_of(g * CHUNK, 16), size)
        return pltpu.make_async_copy(hess_hbm.at[lines], hess.at[g % slots_h, pl.ds(0, size)], load.at[g])

    def side(h):
        return pl.ds(pl.multiple_of(h * half, 64), half)

    def fetch_a(n, own):
        f, size, _ = slots[n] if isinstance(n, int) else ((n - 2) * GROUP, GROUP, GROUP)
        freqs, place = pl.ds(f, size), side(k if own else other)
        return pltpu.make_async_copy(a_hbm.at[freqs, :, place], a.at[freqs, :, place], load_a.at[int(own), n])

    for g in range(slots_h):
        fetch(g, chunk_rows(g)).start()
    for n in [1, *range(2, groups + 2)]:
        fetch_a(n, False).start()

    near = [(dz, dx) for dx in (1, 0) for dz in [*range(1, zs), 0] if dz or dx]
    away = len(near)

    def target(i):
        dz, dx = near[i]
        return at((z + dz) % zs, (x + dx) % 2, c)

    def source(i, cc):
        dz, dx = near[i] if i < away else (0, 0)
        return at((z + zs - dz) % zs, (x + dx) % 2, cc)

    series[...] = jnp.zeros_like(series)
    part[...] = jnp.zeros_like(part)
    m[:, 1] = jnp.zeros_like(m[:, 1])
    barrier = pltpu.get_barrier_semaphore()
    for p in [target(i) for i in range(away)] + [at(z, x, 1 - c)]:
        pl.semaphore_signal(barrier, inc=1, device_id={"wide": p}, device_id_type=MESH)
    pl.semaphore_signal(barrier, inc=1, device_id={"narrow": other}, device_id_type=MESH)
    for b in range(pieces * share):
        own32[b:b + 1, :] = obs_ref[0:1, b * LANES:(b + 1) * LANES].astype(jnp.float32)
    for p in range(pieces):
        mine[p] = own32[p * share:(p + 1) * share].astype(jnp.bfloat16)
    pl.semaphore_wait(barrier, away + 2)

    def share_out(p, i):
        src, slot, dest = (mine.at[p], w, target(i)) if i < away else (
            rows16.at[source(i - away, c), p], source(i - away, c), at(z, x, 1 - c))
        if i == 2 * away:
            src = mine.at[p]
        return pltpu.make_async_remote_copy(
            src_ref=src, dst_ref=rows16.at[slot, p], send_sem=send_o.at[p, i], recv_sem=recv_o.at[p, i],
            device_id={"wide": dest}, device_id_type=MESH)

    for p in range(pieces):
        for i in range(away):
            share_out(p, i).start()
        share_out(p, 2 * away).start()

    def lend(e):
        freqs = pl.ds(moved + e, 1)
        return pltpu.make_async_remote_copy(
            src_ref=a_hbm.at[freqs, :, side(other)], dst_ref=a.at[freqs, :, side(k)],
            send_sem=send_e.at[e], recv_sem=recv_e.at[e], device_id={"narrow": other}, device_id_type=MESH)

    for e in range(LEND):
        lend(e).start()

    def relay(p):
        for i in range(away):
            share_out(p, i).wait_recv()
            share_out(p, away + i).start()

    def place(p, block, slot):
        flat[pl.ds(p * share * scen + slot, share, stride=scen), :] = block.astype(jnp.float32)

    def gather(p):
        place(p, mine[p], w)
        for i in range(away):
            place(p, rows16[source(i, c), p], source(i, c))
        for i in range(away + 1):
            share_out(p, away + i).wait_recv()
            place(p, rows16[source(i, 1 - c), p], source(i, 1 - c))
        for b in range(p * share, (p + 1) * share):
            wide_op[:, b * LANES:(b + 1) * LANES] = flat[b * scen:(b + 1) * scen, :].astype(jnp.bfloat16)

    def across(g):
        return pltpu.make_async_remote_copy(
            src_ref=part.at[g], dst_ref=came.at[g], send_sem=send_n.at[g], recv_sem=recv_n.at[g],
            device_id={"narrow": other}, device_id_type=MESH)

    def dot_rows(g, size, lanes):
        return lax.dot_general(
            wide_op[:, lanes], hess[g % slots_h, 0:size, lanes], (((1,), (1,)), ((), ())),
            preferred_element_type=jnp.float32)

    def product(g, size):
        fetch(g, size).wait()
        part[g, :, 0:size] = dot_rows(g, size, slice(0, cols))

    def merge(g):
        across(g).wait()
        at_lanes = pl.ds(pl.multiple_of(g * CHUNK, LANES), CHUNK)
        series[:, at_lanes] = part[g] + came[g]

    def transform(q):
        windows = []
        first, count = STAGES[q]
        for s in range(first, first + count):
            base = s * nt // LANES * LANES
            window = series[:, base:base + 3 * LANES]
            shift = s * nt - base
            if shift:
                window = pltpu.roll(window, 3 * LANES - shift, 1)
            windows.append(window[:, :2 * LANES])
        got = lax.dot_general(
            jnp.concatenate(windows, axis=0), analysis_ref[k], (((1,), (0,)), ((), ())),
            precision=lax.Precision.HIGHEST, preferred_element_type=jnp.float32).astype(jnp.bfloat16)
        for i in range(count):
            gathered[w * local + first + i, 0:scen] = got[i * scen:(i + 1) * scen, :LANES]
            gathered[w * local + first + i, scen:2 * scen] = got[i * scen:(i + 1) * scen, LANES:]

    def hand(q, i):
        slot, dest = (w, target(i)) if i < away else (source(i - away, c), at(z, x, 1 - c))
        lines = gathered.at[pl.ds(slot * local + STAGES[q][0], STAGES[q][1])]
        return pltpu.make_async_remote_copy(
            src_ref=lines, dst_ref=lines, send_sem=send_s.at[q, i], recv_sem=recv_s.at[q, i],
            device_id={"wide": dest}, device_id_type=MESH)

    def leave(q):
        for i in range(away):
            hand(q, i).start()
        hand(q, 2 * away).start()

    def hop(q):
        for i in range(away):
            hand(q, i).wait_recv()
            hand(q, away + i).start()

    early = 2
    for g in range(early):
        fetch(g, CHUNK).wait()
    relay(0)
    gather(0)
    for p in range(pieces):
        lanes = slice(p * share * LANES, (p + 1) * share * LANES)
        for g in range(early):
            part[g] = part[g] + dot_rows(g, CHUNK, lanes)
            if p + 1 < pieces:
                if g == 0:
                    relay(p + 1)
                if g == early - 1:
                    gather(p + 1)
    for g in range(early):
        fetch(g + slots_h, chunk_rows(g + slots_h)).start()
        across(g).start()
    lend(LEND).start()
    for p in range(pieces):
        for i in range(2 * away + 1):
            share_out(p, i).wait_send()

    def step(g, _):
        product(g, CHUNK)

        @pl.when(g + slots_h < full)
        def _():
            fetch(g + slots_h, CHUNK).start()

        @pl.when(g + slots_h == full)
        def _():
            fetch(full, rest).start()
            for n in [1, *range(2, groups + 2), 0]:
                fetch_a(n, True).start()

        @pl.when(g == 3)
        def _():
            merge(0)
            merge(1)
            transform(0)

        @pl.when(g == 4)
        def _():
            merge(2)

        @pl.when(g == 5)
        def _():
            merge(3)
            transform(1)

        across(g).start()
        lend(LEND + 1 + g - early).start()

        @pl.when(g == 3)
        def _():
            leave(0)

        @pl.when(g == 5)
        def _():
            leave(1)
            hop(0)
        return 0

    lax.fori_loop(early, full, step, 0)
    def finish(q):
        for i in range(away + 1):
            hand(q, away + i).wait_recv()

    def flatten(q):
        first, count = STAGES[q]
        for n in range(scen):
            block = gathered[n * local + first:n * local + first + count]
            start = (n * local + first) * 2 * scen
            flat[start:start + count * 2 * scen, :] = block.reshape(count * 2 * scen, LANES).astype(jnp.float32)

    product(full, rest)
    merge(full - 2)
    across(full).start()
    for e in range(LEND + 1 + full - early, nf - moved):
        lend(e).start()
    transform(2)
    merge(full - 1)
    leave(2)
    transform(3)
    hop(1)
    leave(3)
    height = turned.shape[0] // 32
    unit = (lax.broadcasted_iota(jnp.int32, (height, LANES), 0)
            == lax.broadcasted_iota(jnp.int32, (height, LANES), 1)).astype(jnp.float32).astype(jnp.bfloat16)
    m32[...] = jnp.zeros_like(m32)
    lane = lax.broadcasted_iota(jnp.int32, (8, LANES), 1)
    merge(full)
    transform(4)
    finish(0)
    leave(4)
    flatten(0)
    hop(2)
    finish(1)
    flatten(1)
    hop(3)
    finish(2)
    flatten(2)
    hop(4)
    finish(3)
    flatten(3)
    finish(4)
    flatten(4)

    def turn(n, _):
        both = jnp.concatenate([flat[pl.ds(2 * n + j, sensors, stride=32), :] for j in range(2)], axis=0)
        got = lax.dot_general(unit, both.astype(jnp.bfloat16), (((1,), (1,)), ((), ())),
                              preferred_element_type=jnp.float32)
        for j in range(2):
            turned[pl.ds(2 * n + j, height, stride=32), :] = got[:, j * LANES:(j + 1) * LANES]
        return 0

    lax.fori_loop(0, 16, turn, 0, unroll=4)

    def fill(n, h, dst, lent=False):
        f0, size, high = slots[n] if isinstance(n, int) else ((n - 2) * GROUP, GROUP, GROUP)
        p0 = pl.multiple_of(h * half, 64)
        for i in range(size):
            f = f0 + i
            at_x = nf + i if lent else f
            parts = []
            for e in range(2):
                start = a[f, e, pl.ds(p0, 128), :]
                end = a[f, e, pl.ds(p0 + 128, 64), :]
                parts.append(jnp.concatenate([start, end, end], axis=0))
            re = turned[pl.ds(pl.multiple_of(at_x * 32, 16), 16), :]
            im = turned[pl.ds(pl.multiple_of(at_x * 32 + 16, 16), 16), :]
            xs = jnp.concatenate([jnp.concatenate([re, -im], axis=1), jnp.concatenate([im, re], axis=1)], axis=0)
            got = lax.dot_general(
                xs.astype(jnp.bfloat16), jnp.concatenate(parts, axis=1), (((1,), (1,)), ((), ())),
                preferred_element_type=jnp.float32)
            for e in range(2):
                first, second = got[e * 16:e * 16 + 8], got[e * 16 + 8:e * 16 + 16]
                lines = pl.ds(e * high + i, 8, stride=2 * high)
                m32[0, lines, :] = first[:, :LANES]
                m32[1, lines, :] = second[:, :LANES]
                m32[2, lines, :] = jnp.where(lane < 64, first[:, LANES:], second[:, LANES:])
        for b in range(3):
            block = m32[b, 0:16 * high].reshape(8, 2 * high, LANES)
            dst[:, 0:2 * high, b * LANES:(b + 1) * LANES] = block.astype(jnp.bfloat16)

    def give(n):
        high = slots[n][2] if isinstance(n, int) else GROUP
        lines = pl.ds(0, 2 * high)
        dst = last_ref if isinstance(n, int) and n == groups + 1 else m.at[k, n, :, lines]
        return pltpu.make_async_remote_copy(
            src_ref=sent.at[n, :, lines], dst_ref=dst, send_sem=send_m.at[n], recv_sem=recv_m.at[n],
            device_id={"narrow": other}, device_id_type=MESH)

    def out_first(n, _):
        fetch_a(n, False).wait()
        fill(n, other, sent.at[n])

        @pl.when(n == 2)
        def _():
            give(1).start()

        @pl.when(n > 2)
        def _():
            give(n - 1).start()
        return 0

    fetch_a(1, False).wait()
    fill(1, other, sent.at[1])
    lax.fori_loop(2, groups + 2, out_first, 0)
    fetch_a(1, True).wait()
    fill(1, k, m.at[k, 1])
    give(groups + 1).start()

    def out_own(n, _):
        fetch_a(n, True).wait()
        fill(n, k, m.at[k, n])
        return 0

    lax.fori_loop(2, groups + 2, out_own, 0)
    fetch_a(0, True).wait()
    fill(0, k, m.at[k, 0])
    for e in range(nf - moved):
        lend(e).wait()
    fill(0, other, m.at[other, 0], lent=True)

    def back(which, size, add):
        def one(j, _):
            for lanes, p0 in ((slice(0, 2 * LANES), 0), (slice(2 * LANES, 3 * LANES), LANES)):
                wide = lanes.stop - lanes.start
                got = lax.dot_general(
                    m[which, 0:size, j, :, lanes].reshape(size * 32, wide), synthesis_ref[which, 0:size * 32],
                    (((0,), (0,)), ((), ())), preferred_element_type=jnp.float32)
                for u in range(2):
                    lines = pl.ds(pl.multiple_of((j + 8 * u) * half + p0, 64), wide // 2)
                    for ref, v in ((flat, 0), (turned, 1)):
                        value = got[u * (wide // 2):(u + 1) * (wide // 2), v * LANES:(v + 1) * LANES]
                        ref[lines, :] = ref[lines, :] + value if add else value
            return 0
        lax.fori_loop(0, 8, one, 0)

    back(k, groups + 2, False)
    give(1).wait()

    def drain(n, _):
        give(n).wait()
        return 0

    lax.fori_loop(2, groups + 1, drain, 0)
    back(other, groups + 1, True)
    table_out[...] = synthesis_ref[other, (groups + 1) * 32:(groups + 2) * 32]
    def lay(p, _):
        lines = pl.ds(p, 16, stride=half)
        laid[p, :, 0:LANES] = flat[lines, :]
        laid[p, :, LANES:nt] = turned[lines, :][:, :nt - LANES]
        return 0

    lax.fori_loop(0, half, lay, 0, unroll=4)
    out = pltpu.make_async_copy(laid, base_hbm, leaving)
    out.start()
    for q in range(len(STAGES)):
        for i in range(2 * away + 1):
            hand(q, i).wait_send()
    out.wait()
    give(groups + 1).wait()


def final_kernel(scale, base_hbm, last_hbm, table_hbm, out_hbm, laid, last_ref, table_ref, head, tail, load, sem):
    half, _, nt = out_hbm.shape
    part = half // 3

    def fetch(n):
        lines = pl.ds(n * part, part)
        return pltpu.make_async_copy(base_hbm.at[lines], laid.at[lines], load.at[n])

    def leave(n):
        lines = pl.ds(n * part, part)
        return pltpu.make_async_copy(laid.at[lines], out_hbm.at[lines], sem.at[n])

    small = [pltpu.make_async_copy(last_hbm, last_ref, load.at[3]), pltpu.make_async_copy(table_hbm, table_ref, load.at[4])]
    for cp in small:
        cp.start()
    for n in range(3):
        fetch(n).start()
    for cp in small:
        cp.wait()

    def last(j, lanes, p0):
        got = lax.dot_general(last_ref[j, :, lanes], table_ref[...], (((0,), (0,)), ((), ())),
                              preferred_element_type=jnp.float32)
        wide = (lanes.stop - lanes.start) // 2
        for u in range(2):
            start = (j + 8 * u) * half + p0
            head[start:start + wide] = got[u * wide:(u + 1) * wide, :LANES]
            tail[start:start + wide] = got[u * wide:(u + 1) * wide, LANES:]

    def lay(p, _):
        lines = pl.ds(p, 16, stride=half)
        laid[p, :, 0:LANES] = (laid[p, :, 0:LANES] + head[lines, :]) * scale
        laid[p, :, LANES:nt] = (laid[p, :, LANES:nt] + tail[lines, :][:, :nt - LANES]) * scale
        return 0

    for j in range(8):
        last(j, slice(0, 256), 0)
    for n in range(2):
        fetch(n).wait()
        lax.fori_loop(n * part, (n + 1) * part, lay, 0, unroll=8)
        leave(n).start()
    for j in range(8):
        last(j, slice(256, 384), 128)
    fetch(2).wait()
    lax.fori_loop(2 * part, half, lay, 0, unroll=8)
    leave(2).start()
    for n in range(3):
        leave(n).wait()


def estimate_of(observations, hess, maps, nt, nf, wide):
    rows, cols = hess.shape
    nf_dev, _, points, sensors = maps.shape
    zs, blocks, chunks, stages, pieces, ring = wide // 4, cols // LANES, -(-rows // CHUNK), len(STAGES), 3, 3
    half, n = points // 2, 2 * (2 * zs - 1) + 1
    slots = layout(nf_dev)
    moved = slots[0][0]
    whole = analysis_table(nt, nf).reshape(nt, 2, 2, nf_dev)
    analysis = np.zeros((2, 2 * LANES, 2, LANES), np.float32)
    for k in range(2):
        analysis[k, :nt, :, :nf_dev] = whole[:, :, k]
        analysis[k, :nt, :, nf_dev:nf_dev + EXTRA] = whole[:, :, 1 - k, moved:]
    analysis = analysis.reshape(2, 2 * LANES, 2 * LANES)
    table = synthesis_table(nt, nf).reshape(2, nf_dev, 2, nt)
    synthesis = np.zeros((2, len(slots), 32, 2 * LANES), np.float32)
    for i, (f, size, high) in enumerate(slots):
        for c in range(2):
            synthesis[:, i, c * high:c * high + size, :nt] = table[:, f:f + size, c]
    synthesis = synthesis.reshape(2, len(slots) * 32, 2 * LANES).astype(jnp.bfloat16)
    vm, hb = pl.BlockSpec(memory_space=pltpu.VMEM), pl.BlockSpec(memory_space=pltpu.HBM)
    f32, bf16, dma = jnp.float32, jnp.bfloat16, pltpu.SemaphoreType.DMA
    height = 8 * -(-(nf_dev + EXTRA) // 8)
    parts = pl.pallas_call(
        functools.partial(main_kernel, zs, wide, nt),
        out_shape=[jax.ShapeDtypeStruct((half, 16, nt), f32), jax.ShapeDtypeStruct((8, 32, points), bf16),
                   jax.ShapeDtypeStruct((32, 2 * LANES), bf16)],
        in_specs=[vm, vm, vm, hb, hb], out_specs=[hb, vm, vm],
        scratch_shapes=[
            pltpu.VMEM((ring, CHUNK, cols), bf16), pltpu.VMEM(maps.shape, bf16),
            pltpu.VMEM((blocks, LANES), f32), pltpu.VMEM((pieces, blocks // pieces, LANES), bf16),
            pltpu.VMEM((wide, pieces, blocks // pieces, LANES), bf16),
            pltpu.VMEM((wide, cols), bf16), pltpu.VMEM((chunks, wide, CHUNK), f32),
            pltpu.VMEM((chunks, wide, CHUNK), f32), pltpu.VMEM((wide, chunks * CHUNK), f32),
            pltpu.VMEM((sensors, 2 * wide, LANES), bf16), pltpu.VMEM((sensors * 2 * wide, LANES), f32),
            pltpu.VMEM((height * 32, LANES), f32), pltpu.VMEM((3, 16 * GROUP, LANES), f32),
            pltpu.VMEM((len(slots), 8, 32, points), bf16), pltpu.VMEM((2, len(slots), 8, 32, points), bf16),
            pltpu.VMEM((half, 16, nt), f32),
            dma((chunks,)), dma((2, len(slots))), dma((pieces, n)), dma((pieces, n)), dma((chunks,)), dma((chunks,)),
            dma((stages, n)), dma((stages, n)), dma((len(slots),)), dma((len(slots),)), dma((EXTRA,)), dma((EXTRA,)), dma(()),
        ],
        compiler_params=pltpu.CompilerParams(
            collective_id=0, has_side_effects=True, vmem_limit_bytes=60 << 20),
        name="main",
    )(observations, jnp.asarray(analysis), jnp.asarray(synthesis), hess, maps)
    return pl.pallas_call(
        functools.partial(final_kernel, 1.0 / nf),
        out_shape=jax.ShapeDtypeStruct((half, 16, nt), f32),
        in_specs=[hb] * 3, out_specs=hb,
        scratch_shapes=[pltpu.VMEM((half, 16, nt), f32), pltpu.VMEM((8, 32, points), bf16), pltpu.VMEM((32, 2 * LANES), bf16),
                        pltpu.VMEM((half * 16, LANES), f32),
                        pltpu.VMEM((half * 16, LANES), f32), dma((5,)), dma((3,))],
        compiler_params=pltpu.CompilerParams(vmem_limit_bytes=60 << 20),
        name="final",
    )(*parts)


def per_device(wide, narrow, hess_inverse, observations, adjoint_maps):
    highest = lax.Precision.HIGHEST
    nf_dev, _, points, sensors = adjoint_maps.shape
    nf = nf_dev * narrow
    rows, cols = hess_inverse.shape
    nt = rows * wide // sensors
    scen = observations.shape[0] * wide
    sensors_dev = rows // nt
    tuned = (narrow == 2 and wide == 16 and scen == 16 and sensors == 128 and points == 384
             and cols % LANES == 0 and observations.shape[0] == 1 and rows // CHUNK == 6 and sensors_dev == 8
             and cols // LANES % 3 == 0 and nf_dev == 105)
    table = jnp.asarray(analysis_table(nt, nf))
    if not tuned:
        observed = lax.all_gather(observations, "wide", axis=0, tiled=True)
        values = lax.dot_general(
            observed, hess_inverse, (((1,), (1,)), ((), ())), preferred_element_type=jnp.float32)
        values = values.reshape(scen, sensors_dev, nt)
        terms = jnp.einsum("nst,tcf->sfcn", values, table, precision=highest)
        spectra = lax.psum_scatter(terms, "narrow", scatter_dimension=1, tiled=True).astype(jnp.bfloat16)
        portion = lax.all_gather(spectra, "wide", axis=0, tiled=True)
        both = portion.transpose(1, 2, 3, 0)
        re, im = both[:, 0], both[:, 1]
        x = jnp.concatenate([jnp.concatenate([re, -im], 2), jnp.concatenate([im, re], 2)], 1)
        a = adjoint_maps.transpose(0, 2, 1, 3).reshape(nf_dev, points, 2 * sensors)
        m = jnp.einsum("frk,fpk->frp", x, a, preferred_element_type=jnp.float32).astype(jnp.bfloat16)
        m = m.reshape(nf_dev, 2, scen, points)
        m = lax.all_to_all(m, "narrow", split_axis=3, concat_axis=0, tiled=True)
        est = jnp.einsum("fcnp,fct->ptn", m.astype(jnp.float32), jnp.asarray(synthesis_table(nt, nf)),
                         precision=highest)
        return est * (1.0 / nf)
    return estimate_of(observations, hess_inverse, adjoint_maps, nt, nf, wide).transpose(0, 2, 1)


def solution(mesh):
    wide, narrow = mesh.shape["wide"], mesh.shape["narrow"]
    return jax.shard_map(
        functools.partial(per_device, wide, narrow),
        mesh=mesh,
        in_specs=(P("wide", "narrow"), P("wide", "narrow"), P("narrow", None, "wide", None)),
        out_specs=P(("wide", "narrow"), None, None),
        check_vma=False,
    )
```

```python
import functools
import math

import jax
import jax.numpy as jnp
import numpy as np
from jax import lax
from jax.experimental import pallas as pl
from jax.experimental.pallas import tpu as pltpu
from jax.sharding import PartitionSpec as P

MESH = pl.DeviceIdType.MESH
LANES = 128
CHUNK = 256
GROUP = 16
PITCH = 33
EXTRA = 13
LEND = 4
STAGES = ((0, 2), (2, 2), (4, 2), (6, 1), (7, 1))


def angles(freqs, times, turn):
    return 2.0 * math.pi * ((freqs * times) % turn) / turn


def analysis_table(nt, nf):
    a = angles(np.arange(nt)[:, None], np.arange(nf)[None, :], 2 * nf)
    return np.stack([np.cos(a), -np.sin(a)], axis=1).astype(np.float32)


def synthesis_table(nt, nf):
    a = angles(np.arange(nf)[:, None], np.arange(nt)[None, :], 2 * nf)
    return np.stack([np.cos(a), -np.sin(a)], axis=1).astype(np.float32)


def layout(nf_dev):
    moved = nf_dev - EXTRA
    rest = moved % GROUP
    return [(moved, EXTRA, GROUP), (moved - rest, rest, 4 * -(-rest // 4))] + [
        (f, GROUP, GROUP) for f in range(0, moved - rest, GROUP)]


def main_kernel(zs, scen, nt, obs_hbm, analysis_hbm, synthesis_hbm, hess_hbm, a_hbm, base_hbm, last_ref, table_out,
                obs_ref, analysis_ref, synthesis_ref, hess, a, own32, mine, rows16, wide_op, part, came, series, gathered, flat, turned, m32, sent, m, laid,
                load, load_a, send_o, recv_o, send_n, recv_n, send_s, recv_s, send_m, recv_m, send_e, recv_e,
                leaving, load_t):
    w, k = lax.axis_index("wide"), lax.axis_index("narrow")
    z, x, c = w // 4, (w // 2) % 2, w % 2
    other = 1 - k
    slots_h, _, cols = hess.shape
    pieces, share, _ = mine.shape
    nf, _, points, sensors = a.shape
    half = points // 2
    rows = sensors // scen * nt
    full, rest = rows // CHUNK, rows % CHUNK
    local = rows // nt
    slots = layout(nf)
    moved = slots[0][0]
    groups = len(slots) - 2

    def at(zz, xx, cc):
        return (zz * 2 + xx) * 2 + cc

    def chunk_rows(g):
        return rest if isinstance(g, int) and g == full else CHUNK

    def fetch(g, size):
        lines = pl.ds(pl.multiple_of(g * CHUNK, 16), size)
        return pltpu.make_async_copy(hess_hbm.at[lines], hess.at[g % slots_h, pl.ds(0, size)], load.at[g])

    def side(h):
        return pl.ds(pl.multiple_of(h * half, 64), half)

    def fetch_a(n, own):
        f, size, _ = slots[n] if isinstance(n, int) else ((n - 2) * GROUP, GROUP, GROUP)
        freqs, place = pl.ds(f, size), side(k if own else other)
        return pltpu.make_async_copy(a_hbm.at[freqs, :, place], a.at[freqs, :, place], load_a.at[int(own), n])

    near = [(dz, dx) for dx in (1, 0) for dz in [*range(1, zs), 0] if dz or dx]
    away = len(near)

    def target(i):
        dz, dx = near[i]
        return at((z + dz) % zs, (x + dx) % 2, c)

    def source(i, cc):
        dz, dx = near[i] if i < away else (0, 0)
        return at((z + zs - dz) % zs, (x + dx) % 2, cc)

    barrier = pltpu.get_barrier_semaphore()
    for p in [target(i) for i in range(away)] + [at(z, x, 1 - c)]:
        pl.semaphore_signal(barrier, inc=1, device_id={"wide": p}, device_id_type=MESH)
    pl.semaphore_signal(barrier, inc=1, device_id={"narrow": other}, device_id_type=MESH)
    read = [pltpu.make_async_copy(src, dst, load_t.at[i]) for i, (src, dst) in enumerate(
        [(obs_hbm, obs_ref), (analysis_hbm, analysis_ref), (synthesis_hbm, synthesis_ref)])]
    for cp in read:
        cp.start()
    series[...] = jnp.zeros_like(series)
    part[...] = jnp.zeros_like(part)
    for i in range(2):
        m[i, 1, :, 2 * slots[1][2]:] = jnp.zeros_like(m[i, 1, :, 2 * slots[1][2]:])
    m32[...] = jnp.zeros_like(m32)
    for cp in read:
        cp.wait()
    for g in range(slots_h):
        fetch(g, chunk_rows(g)).start()
    for n in [1, *range(2, groups + 2)]:
        fetch_a(n, False).start()
    for b in range(pieces * share):
        own32[b:b + 1, :] = obs_ref[0:1, b * LANES:(b + 1) * LANES].astype(jnp.float32)
    for p in range(pieces):
        mine[p] = own32[p * share:(p + 1) * share].astype(jnp.bfloat16)
    pl.semaphore_wait(barrier, away + 2)

    def share_out(p, i):
        src, slot, dest = (mine.at[p], w, target(i)) if i < away else (
            rows16.at[source(i - away, c), p], source(i - away, c), at(z, x, 1 - c))
        if i == 2 * away:
            src = mine.at[p]
        return pltpu.make_async_remote_copy(
            src_ref=src, dst_ref=rows16.at[slot, p], send_sem=send_o.at[p, i], recv_sem=recv_o.at[p, i],
            device_id={"wide": dest}, device_id_type=MESH)

    for p in range(pieces):
        for i in range(away):
            share_out(p, i).start()
        share_out(p, 2 * away).start()

    def lend(e):
        freqs = pl.ds(moved + e, 1)
        return pltpu.make_async_remote_copy(
            src_ref=a_hbm.at[freqs, :, side(other)], dst_ref=a.at[freqs, :, side(k)],
            send_sem=send_e.at[e], recv_sem=recv_e.at[e], device_id={"narrow": other}, device_id_type=MESH)

    for e in range(LEND):
        lend(e).start()

    def relay(p):
        for i in range(away):
            share_out(p, i).wait_recv()
            share_out(p, away + i).start()

    def place(p, block, slot):
        flat[pl.ds(p * share * (scen + 1) + slot, share, stride=scen + 1), :] = block.astype(jnp.float32)

    def gather(p):
        place(p, mine[p], w)
        for i in range(away):
            place(p, rows16[source(i, c), p], source(i, c))
        for i in range(away + 1):
            share_out(p, away + i).wait_recv()
            place(p, rows16[source(i, 1 - c), p], source(i, 1 - c))
        for b in range(p * share, (p + 1) * share):
            wide_op[:, b * LANES:(b + 1) * LANES] = flat[b * (scen + 1):b * (scen + 1) + scen, :].astype(jnp.bfloat16)

    def across(g):
        return pltpu.make_async_remote_copy(
            src_ref=part.at[g], dst_ref=came.at[g], send_sem=send_n.at[g], recv_sem=recv_n.at[g],
            device_id={"narrow": other}, device_id_type=MESH)

    def dot_rows(g, size, lanes):
        return lax.dot_general(
            wide_op[:, lanes], hess[g % slots_h, 0:size, lanes], (((1,), (1,)), ((), ())),
            preferred_element_type=jnp.float32)

    def product(g, size):
        fetch(g, size).wait()
        part[g, :, 0:size] = dot_rows(g, size, slice(0, cols))

    def merge(g):
        across(g).wait()
        at_lanes = pl.ds(pl.multiple_of(g * CHUNK, LANES), CHUNK)
        series[:, at_lanes] = part[g] + came[g]

    def transform(q):
        windows = []
        first, count = STAGES[q]
        for s in range(first, first + count):
            base = s * nt // LANES * LANES
            window = series[:, base:base + 3 * LANES]
            shift = s * nt - base
            if shift:
                window = pltpu.roll(window, 3 * LANES - shift, 1)
            windows.append(window[:, :2 * LANES])
        got = lax.dot_general(
            jnp.concatenate(windows, axis=0), analysis_ref[k], (((1,), (0,)), ((), ())),
            precision=lax.Precision.HIGHEST, preferred_element_type=jnp.float32).astype(jnp.bfloat16)
        for i in range(count):
            gathered[w * local + first + i, 0:scen] = got[i * scen:(i + 1) * scen, :LANES]
            gathered[w * local + first + i, scen:2 * scen] = got[i * scen:(i + 1) * scen, LANES:]

    def hand(q, i):
        slot, dest = (w, target(i)) if i < away else (source(i - away, c), at(z, x, 1 - c))
        lines = gathered.at[pl.ds(slot * local + STAGES[q][0], STAGES[q][1])]
        return pltpu.make_async_remote_copy(
            src_ref=lines, dst_ref=lines, send_sem=send_s.at[q, i], recv_sem=recv_s.at[q, i],
            device_id={"wide": dest}, device_id_type=MESH)

    def leave(q):
        for i in range(away):
            hand(q, i).start()
        hand(q, 2 * away).start()

    def hop(q):
        for i in range(away):
            hand(q, i).wait_recv()
            hand(q, away + i).start()

    early = 2
    for g in range(early):
        fetch(g, CHUNK).wait()
    relay(0)
    gather(0)
    for p in range(pieces):
        lanes = slice(p * share * LANES, (p + 1) * share * LANES)
        for g in range(early):
            part[g] = part[g] + dot_rows(g, CHUNK, lanes)
            if p + 1 < pieces:
                if g == 0:
                    relay(p + 1)
                if g == early - 1:
                    gather(p + 1)
            else:
                fetch(g + slots_h, chunk_rows(g + slots_h)).start()
    for g in range(early):
        across(g).start()
    lend(LEND).start()
    for p in range(pieces):
        for i in range(2 * away + 1):
            share_out(p, i).wait_send()

    def step(g, _):
        product(g, CHUNK)

        @pl.when(g + slots_h < full)
        def _():
            fetch(g + slots_h, CHUNK).start()

        @pl.when(g + slots_h == full)
        def _():
            fetch(full, rest).start()
            for n in [1, *range(2, groups + 2), 0]:
                fetch_a(n, True).start()

        @pl.when(g == 3)
        def _():
            merge(0)
            merge(1)
            transform(0)

        @pl.when(g == 4)
        def _():
            merge(2)

        @pl.when(g == 5)
        def _():
            merge(3)
            transform(1)

        across(g).start()
        lend(LEND + 1 + g - early).start()

        @pl.when(g == 3)
        def _():
            leave(0)

        @pl.when(g == 5)
        def _():
            leave(1)
            hop(0)
        return 0

    lax.fori_loop(early, full, step, 0)
    def finish(q):
        for i in range(away + 1):
            hand(q, away + i).wait_recv()

    def flatten(q):
        first, count = STAGES[q]
        for n in range(scen):
            for s in range(n * local + first, n * local + first + count):
                flat[s * PITCH:s * PITCH + 2 * scen, :] = gathered[s].astype(jnp.float32)

    product(full, rest)
    merge(full - 2)
    across(full).start()
    for e in range(LEND + 1 + full - early, nf - moved):
        lend(e).start()
    transform(2)
    merge(full - 1)
    leave(2)
    transform(3)
    hop(1)
    leave(3)
    height = turned.shape[0] // PITCH
    unit = (lax.broadcasted_iota(jnp.int32, (height, LANES), 0)
            == lax.broadcasted_iota(jnp.int32, (height, LANES), 1)).astype(jnp.float32).astype(jnp.bfloat16)
    lane = lax.broadcasted_iota(jnp.int32, (8, LANES), 1)
    merge(full)
    transform(4)
    finish(0)
    leave(4)
    flatten(0)
    hop(2)
    finish(1)
    flatten(1)
    hop(3)
    finish(2)
    flatten(2)
    hop(4)
    finish(3)
    flatten(3)
    finish(4)
    flatten(4)

    def turn(n, _):
        both = jnp.concatenate([flat[pl.ds(2 * n + j, sensors, stride=PITCH), :] for j in range(2)], axis=0)
        got = lax.dot_general(unit, both.astype(jnp.bfloat16), (((1,), (1,)), ((), ())),
                              preferred_element_type=jnp.float32)
        for j in range(2):
            turned[pl.ds(2 * n + j, height, stride=PITCH), :] = got[:, j * LANES:(j + 1) * LANES]
        return 0

    lax.fori_loop(0, 16, turn, 0, unroll=4)

    def fill(n, h, dst, lent=False):
        f0, size, high = slots[n] if isinstance(n, int) else ((n - 2) * GROUP, GROUP, GROUP)
        p0 = pl.multiple_of(h * half, 64)
        for i in range(size):
            f = f0 + i
            at_x = nf + i if lent else f
            parts = []
            for e in range(2):
                start = a[f, e, pl.ds(p0, 128), :]
                end = a[f, e, pl.ds(p0 + 128, 64), :]
                parts.append(jnp.concatenate([start, end, end], axis=0))
            re = turned[pl.ds(at_x * PITCH, 16), :]
            im = turned[pl.ds(at_x * PITCH + 16, 16), :]
            xs = jnp.concatenate([jnp.concatenate([re, -im], axis=1), jnp.concatenate([im, re], axis=1)], axis=0)
            got = lax.dot_general(
                xs.astype(jnp.bfloat16), jnp.concatenate(parts, axis=1), (((1,), (1,)), ((), ())),
                preferred_element_type=jnp.float32)
            for e in range(2):
                first, second = got[e * 16:e * 16 + 8], got[e * 16 + 8:e * 16 + 16]
                lines = pl.ds(e * high + i, 8, stride=2 * high + 1)
                m32[0, lines, :] = first[:, :LANES]
                m32[1, lines, :] = second[:, :LANES]
                m32[2, lines, :] = jnp.where(lane < 64, first[:, LANES:], second[:, LANES:])
        for b in range(3):
            for j in range(8):
                block = m32[b, j * (2 * high + 1):j * (2 * high + 1) + 2 * high]
                dst[j, 0:2 * high, b * LANES:(b + 1) * LANES] = block.astype(jnp.bfloat16)

    def give(n):
        high = slots[n][2] if isinstance(n, int) else GROUP
        lines = pl.ds(0, 2 * high)
        dst = last_ref if isinstance(n, int) and n == groups + 1 else m.at[k, n, :, lines]
        return pltpu.make_async_remote_copy(
            src_ref=sent.at[n, :, lines], dst_ref=dst, send_sem=send_m.at[n], recv_sem=recv_m.at[n],
            device_id={"narrow": other}, device_id_type=MESH)

    def out_first(n, _):
        fetch_a(n, False).wait()
        fill(n, other, sent.at[n])

        @pl.when(n == 2)
        def _():
            give(1).start()

        @pl.when(n > 2)
        def _():
            give(n - 1).start()
        return 0

    fetch_a(1, False).wait()
    fill(1, other, sent.at[1])
    lax.fori_loop(2, groups + 2, out_first, 0)
    fetch_a(1, True).wait()
    fill(1, k, m.at[k, 1])
    give(groups + 1).start()

    def out_own(n, _):
        fetch_a(n, True).wait()
        fill(n, k, m.at[k, n])
        return 0

    lax.fori_loop(2, groups + 2, out_own, 0)
    fetch_a(0, True).wait()
    fill(0, k, m.at[k, 0])
    for e in range(nf - moved):
        lend(e).wait()
    fill(0, other, m.at[other, 0], lent=True)

    def back(which, size, add):
        def one(j, _):
            for lanes, p0 in ((slice(0, 2 * LANES), 0), (slice(2 * LANES, 3 * LANES), LANES)):
                wide = lanes.stop - lanes.start
                got = lax.dot_general(
                    m[which, 0:size, j, :, lanes].reshape(size * 32, wide), synthesis_ref[which, 0:size * 32],
                    (((0,), (0,)), ((), ())), preferred_element_type=jnp.float32)
                for u in range(2):
                    lines = pl.ds(p0 * 17 + j + 8 * u, wide // 2, stride=17)
                    for ref, v in ((flat, 0), (turned, 1)):
                        value = got[u * (wide // 2):(u + 1) * (wide // 2), v * LANES:(v + 1) * LANES]
                        ref[lines, :] = ref[lines, :] + value if add else value
            return 0
        lax.fori_loop(0, 8, one, 0)

    back(k, groups + 2, False)
    give(1).wait()

    def drain(n, _):
        give(n).wait()
        return 0

    lax.fori_loop(2, groups + 1, drain, 0)
    back(other, groups + 1, True)
    table_out[...] = synthesis_ref[other, (groups + 1) * 32:(groups + 2) * 32]
    def lay(p, _):
        lines = pl.ds(p * 17, 16)
        laid[p, :, 0:LANES] = flat[lines, :]
        laid[p, :, LANES:nt] = turned[lines, :][:, :nt - LANES]
        return 0

    lax.fori_loop(0, half, lay, 0, unroll=4)
    out = pltpu.make_async_copy(laid, base_hbm, leaving)
    out.start()
    for q in range(len(STAGES)):
        for i in range(2 * away + 1):
            hand(q, i).wait_send()
    out.wait()
    give(groups + 1).wait()


def final_kernel(scale, base_hbm, last_hbm, table_hbm, out_hbm, laid, last_ref, table_ref, head, tail, load, sem):
    half, _, nt = out_hbm.shape
    part = half // 3

    def fetch(n):
        lines = pl.ds(n * part, part)
        return pltpu.make_async_copy(base_hbm.at[lines], laid.at[lines], load.at[n])

    def leave(n):
        lines = pl.ds(n * part, part)
        return pltpu.make_async_copy(laid.at[lines], out_hbm.at[lines], sem.at[n])

    small = [pltpu.make_async_copy(last_hbm, last_ref, load.at[3]), pltpu.make_async_copy(table_hbm, table_ref, load.at[4])]
    for cp in small:
        cp.start()
    for n in range(3):
        fetch(n).start()
    for cp in small:
        cp.wait()

    def last(j, lanes, p0):
        got = lax.dot_general(last_ref[j, :, lanes], table_ref[...], (((0,), (0,)), ((), ())),
                              preferred_element_type=jnp.float32)
        wide = (lanes.stop - lanes.start) // 2
        for u in range(2):
            lines = pl.ds(p0 * 17 + j + 8 * u, wide, stride=17)
            head[lines, :] = got[u * wide:(u + 1) * wide, :LANES]
            tail[lines, :] = got[u * wide:(u + 1) * wide, LANES:]

    def lay(p, _):
        lines = pl.ds(p * 17, 16)
        laid[p, :, 0:LANES] = (laid[p, :, 0:LANES] + head[lines, :]) * scale
        laid[p, :, LANES:nt] = (laid[p, :, LANES:nt] + tail[lines, :][:, :nt - LANES]) * scale
        return 0

    for j in range(8):
        last(j, slice(0, 256), 0)
    for n in range(2):
        fetch(n).wait()
        lax.fori_loop(n * part, (n + 1) * part, lay, 0, unroll=8)
        leave(n).start()
    for j in range(8):
        last(j, slice(256, 384), 128)
    fetch(2).wait()
    lax.fori_loop(2 * part, half, lay, 0, unroll=8)
    leave(2).start()
    for n in range(3):
        leave(n).wait()


def estimate_of(observations, hess, maps, nt, nf, wide):
    rows, cols = hess.shape
    nf_dev, _, points, sensors = maps.shape
    zs, blocks, chunks, stages, pieces, ring = wide // 4, cols // LANES, -(-rows // CHUNK), len(STAGES), 3, 4
    half, n = points // 2, 2 * (2 * zs - 1) + 1
    slots = layout(nf_dev)
    moved = slots[0][0]
    whole = analysis_table(nt, nf).reshape(nt, 2, 2, nf_dev)
    analysis = np.zeros((2, 2 * LANES, 2, LANES), np.float32)
    for k in range(2):
        analysis[k, :nt, :, :nf_dev] = whole[:, :, k]
        analysis[k, :nt, :, nf_dev:nf_dev + EXTRA] = whole[:, :, 1 - k, moved:]
    analysis = analysis.reshape(2, 2 * LANES, 2 * LANES)
    table = synthesis_table(nt, nf).reshape(2, nf_dev, 2, nt)
    synthesis = np.zeros((2, len(slots), 32, 2 * LANES), np.float32)
    for i, (f, size, high) in enumerate(slots):
        for c in range(2):
            synthesis[:, i, c * high:c * high + size, :nt] = table[:, f:f + size, c]
    synthesis = synthesis.reshape(2, len(slots) * 32, 2 * LANES).astype(jnp.bfloat16)
    vm, hb = pl.BlockSpec(memory_space=pltpu.VMEM), pl.BlockSpec(memory_space=pltpu.HBM)
    f32, bf16, dma = jnp.float32, jnp.bfloat16, pltpu.SemaphoreType.DMA
    height = 8 * -(-(nf_dev + EXTRA) // 8)
    parts = pl.pallas_call(
        functools.partial(main_kernel, zs, wide, nt),
        out_shape=[jax.ShapeDtypeStruct((half, 16, nt), f32), jax.ShapeDtypeStruct((8, 32, points), bf16),
                   jax.ShapeDtypeStruct((32, 2 * LANES), bf16)],
        in_specs=[hb] * 5, out_specs=[hb, vm, vm],
        scratch_shapes=[
            pltpu.VMEM((1, cols), bf16), pltpu.VMEM(analysis.shape, f32), pltpu.VMEM(synthesis.shape, bf16),
            pltpu.VMEM((ring, CHUNK, cols), bf16), pltpu.VMEM(maps.shape, bf16),
            pltpu.VMEM((blocks, LANES), f32), pltpu.VMEM((pieces, blocks // pieces, LANES), bf16),
            pltpu.VMEM((wide, pieces, blocks // pieces, LANES), bf16),
            pltpu.VMEM((wide, cols), bf16), pltpu.VMEM((chunks, wide, CHUNK), f32),
            pltpu.VMEM((chunks, wide, CHUNK), f32), pltpu.VMEM((wide, chunks * CHUNK), f32),
            pltpu.VMEM((sensors, 2 * wide, LANES), bf16), pltpu.VMEM((sensors * PITCH, LANES), f32),
            pltpu.VMEM((height * PITCH, LANES), f32), pltpu.VMEM((3, 8 * PITCH, LANES), f32),
            pltpu.VMEM((len(slots), 8, 32, points), bf16), pltpu.VMEM((2, len(slots), 8, 32, points), bf16),
            pltpu.VMEM((half, 16, nt), f32),
            dma((chunks,)), dma((2, len(slots))), dma((pieces, n)), dma((pieces, n)), dma((chunks,)), dma((chunks,)),
            dma((stages, n)), dma((stages, n)), dma((len(slots),)), dma((len(slots),)), dma((EXTRA,)), dma((EXTRA,)), dma(()), dma((3,)),
        ],
        compiler_params=pltpu.CompilerParams(
            collective_id=0, has_side_effects=True, vmem_limit_bytes=63 << 20),
        name="main",
    )(observations, jnp.asarray(analysis), jnp.asarray(synthesis), hess, maps)
    return pl.pallas_call(
        functools.partial(final_kernel, 1.0 / nf),
        out_shape=jax.ShapeDtypeStruct((half, 16, nt), f32),
        in_specs=[hb] * 3, out_specs=hb,
        scratch_shapes=[pltpu.VMEM((half, 16, nt), f32), pltpu.VMEM((8, 32, points), bf16), pltpu.VMEM((32, 2 * LANES), bf16),
                        pltpu.VMEM((half * 17, LANES), f32),
                        pltpu.VMEM((half * 17, LANES), f32), dma((5,)), dma((3,))],
        compiler_params=pltpu.CompilerParams(vmem_limit_bytes=60 << 20),
        name="final",
    )(*parts)


def per_device(wide, narrow, hess_inverse, observations, adjoint_maps):
    highest = lax.Precision.HIGHEST
    nf_dev, _, points, sensors = adjoint_maps.shape
    nf = nf_dev * narrow
    rows, cols = hess_inverse.shape
    nt = rows * wide // sensors
    scen = observations.shape[0] * wide
    sensors_dev = rows // nt
    tuned = (narrow == 2 and wide == 16 and scen == 16 and sensors == 128 and points == 384
             and cols % LANES == 0 and observations.shape[0] == 1 and rows // CHUNK == 6 and sensors_dev == 8
             and cols // LANES % 3 == 0 and nf_dev == 105)
    table = jnp.asarray(analysis_table(nt, nf))
    if not tuned:
        observed = lax.all_gather(observations, "wide", axis=0, tiled=True)
        values = lax.dot_general(
            observed, hess_inverse, (((1,), (1,)), ((), ())), preferred_element_type=jnp.float32)
        values = values.reshape(scen, sensors_dev, nt)
        terms = jnp.einsum("nst,tcf->sfcn", values, table, precision=highest)
        spectra = lax.psum_scatter(terms, "narrow", scatter_dimension=1, tiled=True).astype(jnp.bfloat16)
        portion = lax.all_gather(spectra, "wide", axis=0, tiled=True)
        both = portion.transpose(1, 2, 3, 0)
        re, im = both[:, 0], both[:, 1]
        x = jnp.concatenate([jnp.concatenate([re, -im], 2), jnp.concatenate([im, re], 2)], 1)
        a = adjoint_maps.transpose(0, 2, 1, 3).reshape(nf_dev, points, 2 * sensors)
        m = jnp.einsum("frk,fpk->frp", x, a, preferred_element_type=jnp.float32).astype(jnp.bfloat16)
        m = m.reshape(nf_dev, 2, scen, points)
        m = lax.all_to_all(m, "narrow", split_axis=3, concat_axis=0, tiled=True)
        est = jnp.einsum("fcnp,fct->ptn", m.astype(jnp.float32), jnp.asarray(synthesis_table(nt, nf)),
                         precision=highest)
        return est * (1.0 / nf)
    return estimate_of(observations, hess_inverse, adjoint_maps, nt, nf, wide).transpose(0, 2, 1)


def solution(mesh):
    wide, narrow = mesh.shape["wide"], mesh.shape["narrow"]
    return jax.shard_map(
        functools.partial(per_device, wide, narrow),
        mesh=mesh,
        in_specs=(P("wide", "narrow"), P("wide", "narrow"), P("narrow", None, "wide", None)),
        out_specs=P(("wide", "narrow"), None, None),
        check_vma=False,
    )
```

```python
import functools
import math

import jax
import jax.numpy as jnp
import numpy as np
from jax import lax
from jax.experimental import pallas as pl
from jax.experimental.pallas import tpu as pltpu
from jax.sharding import PartitionSpec as P

MESH = pl.DeviceIdType.MESH
LANES = 128
CHUNK = 256
GROUP = 16
PITCH = 33
EXTRA = 13
LEND = 4
STAGES = ((0, 2), (2, 2), (4, 2), (6, 1), (7, 1))


def angles(freqs, times, turn):
    return 2.0 * math.pi * ((freqs * times) % turn) / turn


def analysis_table(nt, nf):
    a = angles(np.arange(nt)[:, None], np.arange(nf)[None, :], 2 * nf)
    return np.stack([np.cos(a), -np.sin(a)], axis=1).astype(np.float32)


def synthesis_table(nt, nf):
    a = angles(np.arange(nf)[:, None], np.arange(nt)[None, :], 2 * nf)
    return np.stack([np.cos(a), -np.sin(a)], axis=1).astype(np.float32)


def layout(nf_dev):
    moved = nf_dev - EXTRA
    rest = moved % GROUP
    return [(moved, EXTRA, GROUP), (moved - rest, rest, 4 * -(-rest // 4))] + [
        (f, GROUP, GROUP) for f in range(0, moved - rest, GROUP)]


def main_kernel(zs, scen, nt, obs_hbm, analysis_hbm, synthesis_hbm, hess_hbm, a_hbm, base_hbm, last_ref, table_out,
                obs_ref, analysis_ref, synthesis_ref, hess, a, own32, mine, rows16, wide_op, part, came, series, gathered, flat, turned, m32, sent, m, laid,
                load, load_a, send_o, recv_o, send_n, recv_n, send_s, recv_s, send_m, recv_m, send_e, recv_e,
                leaving, load_t):
    w, k = lax.axis_index("wide"), lax.axis_index("narrow")
    z, x, c = w // 4, (w // 2) % 2, w % 2
    other = 1 - k
    slots_h, _, cols = hess.shape
    pieces, share, _ = mine.shape
    nf, _, points, sensors = a.shape
    half = points // 2
    rows = sensors // scen * nt
    full, rest = rows // CHUNK, rows % CHUNK
    local = rows // nt
    slots = layout(nf)
    moved = slots[0][0]
    groups = len(slots) - 2

    def at(zz, xx, cc):
        return (zz * 2 + xx) * 2 + cc

    def chunk_rows(g):
        return rest if isinstance(g, int) and g == full else CHUNK

    def fetch(g, size):
        lines = pl.ds(pl.multiple_of(g * CHUNK, 16), size)
        return pltpu.make_async_copy(hess_hbm.at[lines], hess.at[g % slots_h, pl.ds(0, size)], load.at[g])

    def side(h):
        return pl.ds(pl.multiple_of(h * half, 64), half)

    def fetch_a(n, own):
        f, size, _ = slots[n] if isinstance(n, int) else ((n - 2) * GROUP, GROUP, GROUP)
        freqs, place = pl.ds(f, size), side(k if own else other)
        return pltpu.make_async_copy(a_hbm.at[freqs, :, place], a.at[freqs, :, place], load_a.at[int(own), n])

    near = [(dz, dx) for dx in (1, 0) for dz in [*range(1, zs), 0] if dz or dx]
    away = len(near)

    def target(i):
        dz, dx = near[i]
        return at((z + dz) % zs, (x + dx) % 2, c)

    def source(i, cc):
        dz, dx = near[i] if i < away else (0, 0)
        return at((z + zs - dz) % zs, (x + dx) % 2, cc)

    barrier = pltpu.get_barrier_semaphore()
    for p in [target(i) for i in range(away)] + [at(z, x, 1 - c)]:
        pl.semaphore_signal(barrier, inc=1, device_id={"wide": p}, device_id_type=MESH)
    pl.semaphore_signal(barrier, inc=1, device_id={"narrow": other}, device_id_type=MESH)
    read = [pltpu.make_async_copy(src, dst, load_t.at[i]) for i, (src, dst) in enumerate(
        [(obs_hbm, obs_ref), (analysis_hbm, analysis_ref), (synthesis_hbm, synthesis_ref)])]
    for cp in read:
        cp.start()
    series[...] = jnp.zeros_like(series)
    part[...] = jnp.zeros_like(part)
    for i in range(2):
        m[i, 1, :, 2 * slots[1][2]:] = jnp.zeros_like(m[i, 1, :, 2 * slots[1][2]:])
    m32[...] = jnp.zeros_like(m32)
    read[0].wait()
    for g in range(slots_h):
        fetch(g, chunk_rows(g)).start()
    for n in [1, *range(2, groups + 2)]:
        fetch_a(n, False).start()
    for b in range(pieces * share):
        own32[b:b + 1, :] = obs_ref[0:1, b * LANES:(b + 1) * LANES].astype(jnp.float32)
    for p in range(pieces):
        mine[p] = own32[p * share:(p + 1) * share].astype(jnp.bfloat16)
    pl.semaphore_wait(barrier, away + 2)

    def share_out(p, i):
        src, slot, dest = (mine.at[p], w, target(i)) if i < away else (
            rows16.at[source(i - away, c), p], source(i - away, c), at(z, x, 1 - c))
        if i == 2 * away:
            src = mine.at[p]
        return pltpu.make_async_remote_copy(
            src_ref=src, dst_ref=rows16.at[slot, p], send_sem=send_o.at[p, i], recv_sem=recv_o.at[p, i],
            device_id={"wide": dest}, device_id_type=MESH)

    for p in range(pieces):
        for i in range(away):
            share_out(p, i).start()
        share_out(p, 2 * away).start()

    def lend(e):
        freqs = pl.ds(moved + e, 1)
        return pltpu.make_async_remote_copy(
            src_ref=a_hbm.at[freqs, :, side(other)], dst_ref=a.at[freqs, :, side(k)],
            send_sem=send_e.at[e], recv_sem=recv_e.at[e], device_id={"narrow": other}, device_id_type=MESH)

    for e in range(LEND):
        lend(e).start()

    def relay(p):
        for i in range(away):
            share_out(p, i).wait_recv()
            share_out(p, away + i).start()

    def place(p, block, slot):
        flat[pl.ds(p * share * (scen + 1) + slot, share, stride=scen + 1), :] = block.astype(jnp.float32)

    def gather(p):
        place(p, mine[p], w)
        for i in range(away):
            place(p, rows16[source(i, c), p], source(i, c))
        for i in range(away + 1):
            share_out(p, away + i).wait_recv()
            place(p, rows16[source(i, 1 - c), p], source(i, 1 - c))
        for b in range(p * share, (p + 1) * share):
            wide_op[:, b * LANES:(b + 1) * LANES] = flat[b * (scen + 1):b * (scen + 1) + scen, :].astype(jnp.bfloat16)

    def across(g):
        return pltpu.make_async_remote_copy(
            src_ref=part.at[g], dst_ref=came.at[g], send_sem=send_n.at[g], recv_sem=recv_n.at[g],
            device_id={"narrow": other}, device_id_type=MESH)

    def dot_rows(g, size, lanes):
        return lax.dot_general(
            wide_op[:, lanes], hess[g % slots_h, 0:size, lanes], (((1,), (1,)), ((), ())),
            preferred_element_type=jnp.float32)

    def product(g, size):
        fetch(g, size).wait()
        part[g, :, 0:size] = dot_rows(g, size, slice(0, cols))

    def merge(g):
        across(g).wait()
        at_lanes = pl.ds(pl.multiple_of(g * CHUNK, LANES), CHUNK)
        series[:, at_lanes] = part[g] + came[g]

    def transform(q):
        windows = []
        first, count = STAGES[q]
        for s in range(first, first + count):
            base = s * nt // LANES * LANES
            window = series[:, base:base + 3 * LANES]
            shift = s * nt - base
            if shift:
                window = pltpu.roll(window, 3 * LANES - shift, 1)
            windows.append(window[:, :2 * LANES])
        whole = jnp.concatenate(windows, axis=0)
        high = whole.astype(jnp.bfloat16)
        low = (whole - high.astype(jnp.float32)).astype(jnp.bfloat16)
        lines = count * scen
        main = lax.dot_general(jnp.concatenate([high, low], axis=0), analysis_ref[k, 0], (((1,), (0,)), ((), ())),
                               preferred_element_type=jnp.float32)
        fine = lax.dot_general(high, analysis_ref[k, 1], (((1,), (0,)), ((), ())), preferred_element_type=jnp.float32)
        got = (main[:lines] + (main[lines:] + fine)).astype(jnp.bfloat16)
        for i in range(count):
            gathered[w * local + first + i, 0:scen] = got[i * scen:(i + 1) * scen, :LANES]
            gathered[w * local + first + i, scen:2 * scen] = got[i * scen:(i + 1) * scen, LANES:]

    def hand(q, i):
        slot, dest = (w, target(i)) if i < away else (source(i - away, c), at(z, x, 1 - c))
        lines = gathered.at[pl.ds(slot * local + STAGES[q][0], STAGES[q][1])]
        return pltpu.make_async_remote_copy(
            src_ref=lines, dst_ref=lines, send_sem=send_s.at[q, i], recv_sem=recv_s.at[q, i],
            device_id={"wide": dest}, device_id_type=MESH)

    def leave(q):
        for i in range(away):
            hand(q, i).start()
        hand(q, 2 * away).start()

    def hop(q):
        for i in range(away):
            hand(q, i).wait_recv()
            hand(q, away + i).start()

    early = 2
    for g in range(early):
        fetch(g, CHUNK).wait()
    relay(0)
    gather(0)
    for p in range(pieces):
        lanes = slice(p * share * LANES, (p + 1) * share * LANES)
        for g in range(early):
            part[g] = part[g] + dot_rows(g, CHUNK, lanes)
            if p + 1 < pieces:
                if g == 0:
                    relay(p + 1)
                if g == early - 1:
                    gather(p + 1)
            else:
                fetch(g + slots_h, chunk_rows(g + slots_h)).start()
    for g in range(early):
        across(g).start()
    lend(LEND).start()
    for p in range(pieces):
        for i in range(2 * away + 1):
            share_out(p, i).wait_send()

    def step(g, _):
        product(g, CHUNK)

        @pl.when(g + slots_h < full)
        def _():
            fetch(g + slots_h, CHUNK).start()

        @pl.when(g + slots_h == full)
        def _():
            fetch(full, rest).start()
            for n in [1, *range(2, groups + 2), 0]:
                fetch_a(n, True).start()

        @pl.when(g == 3)
        def _():
            merge(0)
            merge(1)
            transform(0)

        @pl.when(g == 4)
        def _():
            merge(2)

        @pl.when(g == 5)
        def _():
            merge(3)
            transform(1)

        across(g).start()
        lend(LEND + 1 + g - early).start()

        @pl.when(g == 3)
        def _():
            leave(0)

        @pl.when(g == 5)
        def _():
            leave(1)
            hop(0)
        return 0

    for cp in read[1:]:
        cp.wait()
    lax.fori_loop(early, full, step, 0)
    def finish(q):
        for i in range(away + 1):
            hand(q, away + i).wait_recv()

    def flatten(q):
        first, count = STAGES[q]
        for n in range(scen):
            for s in range(n * local + first, n * local + first + count):
                flat[s * PITCH:s * PITCH + 2 * scen, :] = gathered[s].astype(jnp.float32)

    product(full, rest)
    merge(full - 2)
    across(full).start()
    for e in range(LEND + 1 + full - early, nf - moved):
        lend(e).start()
    transform(2)
    merge(full - 1)
    leave(2)
    transform(3)
    hop(1)
    leave(3)
    height = turned.shape[0] // PITCH
    unit = (lax.broadcasted_iota(jnp.int32, (height, LANES), 0)
            == lax.broadcasted_iota(jnp.int32, (height, LANES), 1)).astype(jnp.float32).astype(jnp.bfloat16)
    lane = lax.broadcasted_iota(jnp.int32, (8, LANES), 1)
    merge(full)
    transform(4)
    finish(0)
    leave(4)
    flatten(0)
    hop(2)
    finish(1)
    flatten(1)
    hop(3)
    finish(2)
    flatten(2)
    hop(4)
    finish(3)
    flatten(3)
    finish(4)
    flatten(4)

    def turn(n, _):
        both = jnp.concatenate([flat[pl.ds(2 * n + j, sensors, stride=PITCH), :] for j in range(2)], axis=0)
        got = lax.dot_general(unit, both.astype(jnp.bfloat16), (((1,), (1,)), ((), ())),
                              preferred_element_type=jnp.float32)
        for j in range(2):
            turned[pl.ds(2 * n + j, height, stride=PITCH), :] = got[:, j * LANES:(j + 1) * LANES]
        return 0

    lax.fori_loop(0, 16, turn, 0, unroll=4)

    def fill(n, h, dst, lent=False):
        f0, size, high = slots[n] if isinstance(n, int) else ((n - 2) * GROUP, GROUP, GROUP)
        p0 = pl.multiple_of(h * half, 64)
        for i in range(size):
            f = f0 + i
            at_x = nf + i if lent else f
            parts = []
            for e in range(2):
                start = a[f, e, pl.ds(p0, 128), :]
                end = a[f, e, pl.ds(p0 + 128, 64), :]
                parts.append(jnp.concatenate([start, end, end], axis=0))
            re = turned[pl.ds(at_x * PITCH, 16), :]
            im = turned[pl.ds(at_x * PITCH + 16, 16), :]
            xs = jnp.concatenate([jnp.concatenate([re, -im], axis=1), jnp.concatenate([im, re], axis=1)], axis=0)
            got = lax.dot_general(
                xs.astype(jnp.bfloat16), jnp.concatenate(parts, axis=1), (((1,), (1,)), ((), ())),
                preferred_element_type=jnp.float32)
            for e in range(2):
                first, second = got[e * 16:e * 16 + 8], got[e * 16 + 8:e * 16 + 16]
                lines = pl.ds(e * high + i, 8, stride=2 * high + 1)
                m32[0, lines, :] = first[:, :LANES]
                m32[1, lines, :] = second[:, :LANES]
                m32[2, lines, :] = jnp.where(lane < 64, first[:, LANES:], second[:, LANES:])
        for b in range(3):
            for j in range(8):
                block = m32[b, j * (2 * high + 1):j * (2 * high + 1) + 2 * high]
                dst[j, 0:2 * high, b * LANES:(b + 1) * LANES] = block.astype(jnp.bfloat16)

    def give(n):
        high = slots[n][2] if isinstance(n, int) else GROUP
        lines = pl.ds(0, 2 * high)
        dst = last_ref if isinstance(n, int) and n == groups + 1 else m.at[k, n, :, lines]
        return pltpu.make_async_remote_copy(
            src_ref=sent.at[n, :, lines], dst_ref=dst, send_sem=send_m.at[n], recv_sem=recv_m.at[n],
            device_id={"narrow": other}, device_id_type=MESH)

    def out_first(n, _):
        fetch_a(n, False).wait()
        fill(n, other, sent.at[n])

        @pl.when(n == 2)
        def _():
            give(1).start()

        @pl.when(n > 2)
        def _():
            give(n - 1).start()
        return 0

    fetch_a(1, False).wait()
    fill(1, other, sent.at[1])
    lax.fori_loop(2, groups + 2, out_first, 0)
    fetch_a(1, True).wait()
    fill(1, k, m.at[k, 1])
    give(groups + 1).start()

    def out_own(n, _):
        fetch_a(n, True).wait()
        fill(n, k, m.at[k, n])
        return 0

    lax.fori_loop(2, groups + 2, out_own, 0)
    fetch_a(0, True).wait()
    fill(0, k, m.at[k, 0])
    for e in range(nf - moved):
        lend(e).wait()
    fill(0, other, m.at[other, 0], lent=True)

    def back(which, size, add):
        def one(j, _):
            for lanes, p0 in ((slice(0, 2 * LANES), 0), (slice(2 * LANES, 3 * LANES), LANES)):
                wide = lanes.stop - lanes.start
                got = lax.dot_general(
                    m[which, 0:size, j, :, lanes].reshape(size * 32, wide), synthesis_ref[which, 0:size * 32],
                    (((0,), (0,)), ((), ())), preferred_element_type=jnp.float32)
                for u in range(2):
                    lines = pl.ds(p0 * 17 + j + 8 * u, wide // 2, stride=17)
                    for ref, v in ((flat, 0), (turned, 1)):
                        value = got[u * (wide // 2):(u + 1) * (wide // 2), v * LANES:(v + 1) * LANES]
                        ref[lines, :] = ref[lines, :] + value if add else value
            return 0
        lax.fori_loop(0, 8, one, 0)

    back(k, groups + 2, False)
    give(1).wait()

    def drain(n, _):
        give(n).wait()
        return 0

    lax.fori_loop(2, groups + 1, drain, 0)
    back(other, groups + 1, True)
    table_out[...] = synthesis_ref[other, (groups + 1) * 32:(groups + 2) * 32]
    def lay(p, _):
        lines = pl.ds(p * 17, 16)
        laid[p, :, 0:LANES] = flat[lines, :]
        laid[p, :, LANES:nt] = turned[lines, :][:, :nt - LANES]
        return 0

    lax.fori_loop(0, half, lay, 0, unroll=4)
    out = pltpu.make_async_copy(laid, base_hbm, leaving)
    out.start()
    for q in range(len(STAGES)):
        for i in range(2 * away + 1):
            hand(q, i).wait_send()
    out.wait()
    give(groups + 1).wait()


def final_kernel(scale, base_hbm, last_hbm, table_hbm, out_hbm, laid, last_ref, table_ref, head, tail, load, sem):
    half, _, nt = out_hbm.shape
    part = half // 6

    def fetch(n):
        lines = pl.ds(n * part, part)
        return pltpu.make_async_copy(base_hbm.at[lines], laid.at[lines], load.at[n])

    def leave(n):
        lines = pl.ds(n * part, part)
        return pltpu.make_async_copy(laid.at[lines], out_hbm.at[lines], sem.at[n])

    small = [pltpu.make_async_copy(last_hbm, last_ref, load.at[6]), pltpu.make_async_copy(table_hbm, table_ref, load.at[7])]
    for cp in small:
        cp.start()
    for n in range(6):
        fetch(n).start()
    for cp in small:
        cp.wait()

    def last(j, lanes, p0):
        got = lax.dot_general(last_ref[j, :, lanes], table_ref[...], (((0,), (0,)), ((), ())),
                              preferred_element_type=jnp.float32)
        wide = (lanes.stop - lanes.start) // 2
        for u in range(2):
            lines = pl.ds(p0 * 17 + j + 8 * u, wide, stride=17)
            head[lines, :] = got[u * wide:(u + 1) * wide, :LANES]
            tail[lines, :] = got[u * wide:(u + 1) * wide, LANES:]

    def lay(p, _):
        lines = pl.ds(p * 17, 16)
        laid[p, :, 0:LANES] = (laid[p, :, 0:LANES] + head[lines, :]) * scale
        laid[p, :, LANES:nt] = (laid[p, :, LANES:nt] + tail[lines, :][:, :nt - LANES]) * scale
        return 0

    for j in range(8):
        last(j, slice(0, 256), 0)
        last(j, slice(256, 384), 128)
    for n in range(6):
        fetch(n).wait()
        lax.fori_loop(n * part, (n + 1) * part, lay, 0, unroll=8)
        leave(n).start()
    for n in range(6):
        leave(n).wait()


def estimate_of(observations, hess, maps, nt, nf, wide):
    rows, cols = hess.shape
    nf_dev, _, points, sensors = maps.shape
    zs, blocks, chunks, stages, pieces, ring = wide // 4, cols // LANES, -(-rows // CHUNK), len(STAGES), 3, 4
    half, n = points // 2, 2 * (2 * zs - 1) + 1
    slots = layout(nf_dev)
    moved = slots[0][0]
    whole = analysis_table(nt, nf).reshape(nt, 2, 2, nf_dev)
    analysis = np.zeros((2, 2 * LANES, 2, LANES), np.float32)
    for k in range(2):
        analysis[k, :nt, :, :nf_dev] = whole[:, :, k]
        analysis[k, :nt, :, nf_dev:nf_dev + EXTRA] = whole[:, :, 1 - k, moved:]
    analysis = analysis.reshape(2, 2 * LANES, 2 * LANES)
    coarse = analysis.astype(jnp.bfloat16)
    analysis = np.stack([coarse, (analysis - coarse.astype(np.float32)).astype(jnp.bfloat16)], axis=1)
    table = synthesis_table(nt, nf).reshape(2, nf_dev, 2, nt)
    synthesis = np.zeros((2, len(slots), 32, 2 * LANES), np.float32)
    for i, (f, size, high) in enumerate(slots):
        for c in range(2):
            synthesis[:, i, c * high:c * high + size, :nt] = table[:, f:f + size, c]
    synthesis = synthesis.reshape(2, len(slots) * 32, 2 * LANES).astype(jnp.bfloat16)
    vm, hb = pl.BlockSpec(memory_space=pltpu.VMEM), pl.BlockSpec(memory_space=pltpu.HBM)
    f32, bf16, dma = jnp.float32, jnp.bfloat16, pltpu.SemaphoreType.DMA
    height = 8 * -(-(nf_dev + EXTRA) // 8)
    parts = pl.pallas_call(
        functools.partial(main_kernel, zs, wide, nt),
        out_shape=[jax.ShapeDtypeStruct((half, 16, nt), f32), jax.ShapeDtypeStruct((8, 32, points), bf16),
                   jax.ShapeDtypeStruct((32, 2 * LANES), bf16)],
        in_specs=[hb] * 5, out_specs=[hb, vm, vm],
        scratch_shapes=[
            pltpu.VMEM((1, cols), bf16), pltpu.VMEM(analysis.shape, bf16), pltpu.VMEM(synthesis.shape, bf16),
            pltpu.VMEM((ring, CHUNK, cols), bf16), pltpu.VMEM(maps.shape, bf16),
            pltpu.VMEM((blocks, LANES), f32), pltpu.VMEM((pieces, blocks // pieces, LANES), bf16),
            pltpu.VMEM((wide, pieces, blocks // pieces, LANES), bf16),
            pltpu.VMEM((wide, cols), bf16), pltpu.VMEM((chunks, wide, CHUNK), f32),
            pltpu.VMEM((chunks, wide, CHUNK), f32), pltpu.VMEM((wide, chunks * CHUNK), f32),
            pltpu.VMEM((sensors, 2 * wide, LANES), bf16), pltpu.VMEM((sensors * PITCH, LANES), f32),
            pltpu.VMEM((height * PITCH, LANES), f32), pltpu.VMEM((3, 8 * PITCH, LANES), f32),
            pltpu.VMEM((len(slots), 8, 32, points), bf16), pltpu.VMEM((2, len(slots), 8, 32, points), bf16),
            pltpu.VMEM((half, 16, nt), f32),
            dma((chunks,)), dma((2, len(slots))), dma((pieces, n)), dma((pieces, n)), dma((chunks,)), dma((chunks,)),
            dma((stages, n)), dma((stages, n)), dma((len(slots),)), dma((len(slots),)), dma((EXTRA,)), dma((EXTRA,)), dma(()), dma((3,)),
        ],
        compiler_params=pltpu.CompilerParams(
            collective_id=0, has_side_effects=True, vmem_limit_bytes=63 << 20),
        name="main",
    )(observations, jnp.asarray(analysis), jnp.asarray(synthesis), hess, maps)
    return pl.pallas_call(
        functools.partial(final_kernel, 1.0 / nf),
        out_shape=jax.ShapeDtypeStruct((half, 16, nt), f32),
        in_specs=[hb] * 3, out_specs=hb,
        scratch_shapes=[pltpu.VMEM((half, 16, nt), f32), pltpu.VMEM((8, 32, points), bf16), pltpu.VMEM((32, 2 * LANES), bf16),
                        pltpu.VMEM((half * 17, LANES), f32),
                        pltpu.VMEM((half * 17, LANES), f32), dma((8,)), dma((6,))],
        compiler_params=pltpu.CompilerParams(vmem_limit_bytes=60 << 20),
        name="final",
    )(*parts)


def per_device(wide, narrow, hess_inverse, observations, adjoint_maps):
    highest = lax.Precision.HIGHEST
    nf_dev, _, points, sensors = adjoint_maps.shape
    nf = nf_dev * narrow
    rows, cols = hess_inverse.shape
    nt = rows * wide // sensors
    scen = observations.shape[0] * wide
    sensors_dev = rows // nt
    tuned = (narrow == 2 and wide == 16 and scen == 16 and sensors == 128 and points == 384
             and cols % LANES == 0 and observations.shape[0] == 1 and rows // CHUNK == 6 and sensors_dev == 8
             and cols // LANES % 3 == 0 and nf_dev == 105)
    table = jnp.asarray(analysis_table(nt, nf))
    if not tuned:
        observed = lax.all_gather(observations, "wide", axis=0, tiled=True)
        values = lax.dot_general(
            observed, hess_inverse, (((1,), (1,)), ((), ())), preferred_element_type=jnp.float32)
        values = values.reshape(scen, sensors_dev, nt)
        terms = jnp.einsum("nst,tcf->sfcn", values, table, precision=highest)
        spectra = lax.psum_scatter(terms, "narrow", scatter_dimension=1, tiled=True).astype(jnp.bfloat16)
        portion = lax.all_gather(spectra, "wide", axis=0, tiled=True)
        both = portion.transpose(1, 2, 3, 0)
        re, im = both[:, 0], both[:, 1]
        x = jnp.concatenate([jnp.concatenate([re, -im], 2), jnp.concatenate([im, re], 2)], 1)
        a = adjoint_maps.transpose(0, 2, 1, 3).reshape(nf_dev, points, 2 * sensors)
        m = jnp.einsum("frk,fpk->frp", x, a, preferred_element_type=jnp.float32).astype(jnp.bfloat16)
        m = m.reshape(nf_dev, 2, scen, points)
        m = lax.all_to_all(m, "narrow", split_axis=3, concat_axis=0, tiled=True)
        est = jnp.einsum("fcnp,fct->ptn", m.astype(jnp.float32), jnp.asarray(synthesis_table(nt, nf)),
                         precision=highest)
        return est * (1.0 / nf)
    return estimate_of(observations, hess_inverse, adjoint_maps, nt, nf, wide).transpose(0, 2, 1)


def solution(mesh):
    wide, narrow = mesh.shape["wide"], mesh.shape["narrow"]
    return jax.shard_map(
        functools.partial(per_device, wide, narrow),
        mesh=mesh,
        in_specs=(P("wide", "narrow"), P("wide", "narrow"), P("narrow", None, "wide", None)),
        out_specs=P(("wide", "narrow"), None, None),
        check_vma=False,
    )
```
